32 devices in a mesh: tm: 8 (over z, x), rows: 4 (over y, core).
Axes of the slice: x: 2, y: 2, z: 4, core: 2. Of those that a mesh axis runs over, the one named last changes fastest.
Arguments:
- video: bfloat16 [128, 32, 32, 512], P('tm', 'rows'), may hold values from -6 to 6
- video_ids: int32 [128], replicated, may hold values from 0 to 7, never falling along the last dimension, each value on 1 to 32 neighbouring positions
- w_space: bfloat16 [9, 512, 512], replicated, may hold values from -0.09375 to 0.09375
- w_time: bfloat16 [3, 512, 512], replicated, may hold values from -0.15625 to 0.15625
- spatial_attn: bfloat16 [4, 512, 512], replicated, may hold values from -2 to 2, as said below
- time_attn: bfloat16 [4, 512, 512], replicated, may hold values from -2 to 2, as said below
Outputs:
- mixed: bfloat16 [128, 32, 32, 512], P(None, 'rows', 'tm')
The draws below stay inside these ranges and needn't reach their ends.
Inputs may be any that keep to these rules, and one draw needn't show every extreme that they name: `spatial_attn`: Query, key, value and output projections stacked in this order. `time_attn`: Query, key, value and output projections stacked in this order.
All inputs are finite; a program needn't handle non-finite values.
Results may differ from the reference program's by a relative error of at most 0.024.
The reference program's roundings to bfloat16 on the way count: a program that leaves them out, or rounds other values in their place, can miss the bound.
Values may be sent and summed in bfloat16 or wider, within the bound.
A program may use at most 128 MiB of HBM per device.

```python
import math
import jax
import jax.numpy as jnp
import numpy as np
from jax import lax

C = 512
H = 32
W = 32
GROUPS = 32
LONGEST = 32
FRAMES = 128
VIDEOS = 8


def stacked_projections(key):
    first = jax.random.fold_in(key, 0)
    weights = jax.random.normal(first, (4, C, C), jnp.float32) / jnp.sqrt(jnp.float32(C))
    return jnp.clip(weights, -2.0, 2.0).astype(jnp.bfloat16)


def draw_spatial_attn(key, part):
    return stacked_projections(jax.random.fold_in(key, 101))


def draw_time_attn(key, part):
    return stacked_projections(jax.random.fold_in(key, 202))


def block_levels(stream_key, dims, pieces, smallest, top_value):
    gain, own = 1.0, jax.random.fold_in(stream_key, 6)
    for dim, blocks in pieces:
        draws = jnp.exp(jax.random.uniform(jax.random.fold_in(own, dim), (blocks,), jnp.float32, smallest / len(pieces), top_value / len(pieces)))
        gain = gain * jnp.repeat(draws, dims[dim] // blocks).reshape([-1 if axis == dim else 1 for axis in range(len(dims))])
    return gain


def split_up(amount, total, reach, slope):
    weights = [(1 << 20) // math.isqrt(grade ** slope) + 1 for grade in range(2, amount + 1)]
    surplus, counts = total - reach - (amount - 1), [1] * (amount - 1)
    while surplus > 0:
        movable = [i for i in range(amount - 1) if counts[i] < reach]
        pool, left = sum([weights[i] for i in movable]), surplus
        for i in movable:
            addition = min(reach - counts[i], max(1, left * weights[i] // pool), surplus)
            counts[i] = counts[i] + addition
            surplus = surplus - addition
    return np.array([reach] + counts)


def ragged(own_key, amount, total, bound, lean):
    if amount == 2:
        one = jax.random.randint(own_key, (), max(1, total - bound), min(bound, total - 1) + 1)
        return jnp.stack([one, total - one])
    lengths = jnp.asarray(split_up(amount, total, bound, lean), jnp.int32)
    twos = (amount - 1) // 2
    source_of, taker = lengths[1:1 + 2 * twos:2], lengths[2:2 + 2 * twos:2]
    slack = jnp.minimum(source_of - 1, bound - taker)
    passed = jax.random.randint(jax.random.fold_in(own_key, 1), (twos,), 0, 1 << 20) % (slack + 1)
    lengths = lengths.at[1:1 + 2 * twos:2].set(source_of - passed).at[2:2 + 2 * twos:2].set(taker + passed)
    return lengths[jax.random.permutation(jax.random.fold_in(own_key, 2), amount)]


def normal_values(rng, shape, scale, limit, cuts=(), kind=jnp.bfloat16):
    values = scale * jax.random.normal(rng, shape, jnp.float32)
    if cuts:
        values = values * block_levels(rng, shape, cuts, -0.22, 0.18)
    return jnp.clip(values, -limit, limit).astype(kind)


def setup_inputs(seed: int = 0) -> dict:
    seeds = jax.random.split(jax.random.key(seed), 7)
    video = normal_values(seeds[0], (FRAMES, H, W, C), 1.0, 6.0, ((0, 8), (1, 4)))
    video_ids = jnp.searchsorted(jnp.cumsum(ragged(seeds[1], VIDEOS, FRAMES, LONGEST, 2)), jnp.arange(FRAMES), side="right").astype(jnp.int32)
    w_space = normal_values(seeds[2], (9, C, C), (9 * C) ** -0.5, 0.09375)
    w_time = normal_values(seeds[3], (3, C, C), (3 * C) ** -0.5, 0.15625)
    spatial_attn = draw_spatial_attn(jax.random.fold_in(seeds[6], 71), 0)
    time_attn = draw_time_attn(jax.random.fold_in(seeds[6], 71), 0)
    return {"video": video, "video_ids": video_ids, "w_space": w_space, "w_time": w_time, "spatial_attn": spatial_attn, "time_attn": time_attn}


epsilon = 1e-06
masked_score = -1e+30

def space_conv(video, weights):
    frame_count, row_count, col_count, channel_width = video.shape
    widened = jnp.pad(video, ((0, 0), (1, 1), (1, 1), (0, 0)))
    summed = jnp.zeros((frame_count * row_count * col_count, channel_width), jnp.float32)
    for row_shift in range(3):
        for col_shift in range(3):
            window = widened[:, row_shift:row_shift + row_count, col_shift:col_shift + col_count, :]
            summed = summed + jnp.dot(window.reshape(-1, channel_width), weights[row_shift * 3 + col_shift], preferred_element_type=jnp.float32)
    return summed.reshape(video.shape)

def time_taps(hidden, video_ids):
    frame_total = hidden.shape[0]
    frame_index = jnp.arange(frame_total, dtype=jnp.int32)
    back_one = jnp.maximum(frame_index - 1, 0).astype(jnp.int32)
    back_two = jnp.maximum(frame_index - 2, 0).astype(jnp.int32)
    prev_one = jnp.where((frame_index >= 1) & (video_ids[back_one] == video_ids), back_one, frame_index)
    prev_two = jnp.where((frame_index >= 2) & (video_ids[back_two] == video_ids), back_two, prev_one)
    return (jnp.take(hidden, prev_one, axis=0), jnp.take(hidden, prev_two, axis=0))

def group_norm(tokens, groups):
    batch_size, length, channel_width = tokens.shape
    per_group = channel_width // groups
    values = tokens.astype(jnp.float32)
    group_sums = lax.optimization_barrier(jnp.sum(values, axis=1)).reshape(batch_size, groups, per_group).sum(axis=2)
    squares = lax.optimization_barrier(jnp.sum(values * values, axis=1)).reshape(batch_size, groups, per_group).sum(axis=2)
    entries = length * per_group
    average = group_sums / entries
    spread = squares / entries - average * average
    inverse = lax.rsqrt(spread + epsilon)
    average_full = jnp.repeat(average, per_group, axis=1)[:, None, :]
    inverse_full = jnp.repeat(inverse, per_group, axis=1)[:, None, :]
    return ((values - average_full) * inverse_full).astype(jnp.bfloat16)

def project(normed, weights):
    shape_in = normed.shape
    channel_width = shape_in[-1]
    flattened = normed.reshape(-1, channel_width)
    outputs = [jnp.dot(flattened, weights[index], preferred_element_type=jnp.float32).astype(jnp.bfloat16).reshape(shape_in) for index in range(3)]
    return (outputs[0], outputs[1], outputs[2])

def frame_attention(tokens, normed, weights):
    channel_width = tokens.shape[-1]
    query_rows, resident_keys, resident_values = project(normed, weights)
    attention_logits = jnp.einsum('edm,efm->edf', query_rows.astype(jnp.float32), resident_keys.astype(jnp.float32)) * channel_width ** (-0.5)
    top = lax.optimization_barrier(jnp.max(attention_logits, axis=-1, keepdims=True))
    raised = jnp.exp(attention_logits - top)
    attention_probs = (raised / lax.optimization_barrier(jnp.sum(raised, axis=-1, keepdims=True))).astype(jnp.bfloat16)
    mixed_output = jnp.einsum('lup,lpe->lue', attention_probs.astype(jnp.float32), resident_values.astype(jnp.float32)).astype(jnp.bfloat16)
    output = tokens.astype(jnp.float32) + jnp.dot(mixed_output.reshape(-1, channel_width), weights[3], preferred_element_type=jnp.float32).reshape(tokens.shape)
    return output.astype(jnp.bfloat16)

def time_attention(column_block, video_ids, weights):
    frame_total, positions, channel_width = column_block.shape
    values = column_block.astype(jnp.float32)
    average = lax.optimization_barrier(jnp.mean(values, axis=-1, keepdims=True))
    centered = values - average
    spread = lax.optimization_barrier(jnp.mean(centered * centered, axis=-1, keepdims=True))
    normed = (centered * lax.rsqrt(spread + epsilon)).astype(jnp.bfloat16)
    query_rows, resident_keys, resident_values = project(normed, weights)
    attention_logits = jnp.einsum('fpc,gpc->pfg', query_rows.astype(jnp.float32), resident_keys.astype(jnp.float32)) * channel_width ** (-0.5)
    frame_index = jnp.arange(frame_total, dtype=jnp.int32)
    allowed = (frame_index[None, :] <= frame_index[:, None]) & (video_ids[None, :] == video_ids[:, None])
    attention_logits = jnp.where(allowed[None], attention_logits, masked_score)
    top = lax.optimization_barrier(jnp.max(attention_logits, axis=-1, keepdims=True))
    raised = jnp.exp(attention_logits - top)
    attention_probs = (raised / lax.optimization_barrier(jnp.sum(raised, axis=-1, keepdims=True))).astype(jnp.bfloat16)
    mixed_output = jnp.einsum('pfg,gpc->fpc', attention_probs.astype(jnp.float32), resident_values.astype(jnp.float32)).astype(jnp.bfloat16)
    output = values + jnp.dot(mixed_output.reshape(-1, channel_width), weights[3], preferred_element_type=jnp.float32).reshape(column_block.shape)
    return output.astype(jnp.bfloat16)

def reference(video, video_ids, w_space, w_time, spatial_attn, time_attn):
    frame_count, row_count, col_count, channel_width = video.shape
    hidden = jax.nn.silu(space_conv(video, w_space)).astype(jnp.bfloat16)
    prev_one, prev_two = time_taps(hidden, video_ids)
    temporal = jnp.dot(hidden.reshape(-1, channel_width), w_time[0], preferred_element_type=jnp.float32)
    temporal = temporal + jnp.dot(prev_one.reshape(-1, channel_width), w_time[1], preferred_element_type=jnp.float32)
    temporal = temporal + jnp.dot(prev_two.reshape(-1, channel_width), w_time[2], preferred_element_type=jnp.float32)
    conv_out = (video.astype(jnp.float32) + temporal.reshape(video.shape)).astype(jnp.bfloat16)
    tokens = conv_out.reshape(frame_count, row_count * col_count, channel_width)
    normed = group_norm(tokens, GROUPS)

    def one_frame(paired):
        return frame_attention(paired[0][None], paired[1][None], spatial_attn)[0]
    frame_out = lax.map(one_frame, (tokens, normed)).reshape(video.shape)
    columns = jnp.moveaxis(frame_out, 1, 0)

    def one_row(column_block):
        return time_attention(column_block, video_ids, time_attn)
    by_time = lax.map(one_row, columns)
    return jnp.moveaxis(by_time, 0, 1)
```

```python
import jax
import jax.numpy as jnp
from jax import lax
from jax.experimental import pallas as pl
from jax.experimental.pallas import tpu as pltpu
from jax.sharding import PartitionSpec as P

GROUPS = 32
epsilon = 1e-06
masked_score = -1e30
f32, bf16 = jnp.float32, jnp.bfloat16
VMEM_LIMIT = 60 * 1024 * 1024


def dot32(a, b):
    return jnp.dot(a, b, preferred_element_type=f32)


def conv_hidden(padded, w_ref, frames, rows, cols, chans):
    m = frames * rows * cols
    col = lax.broadcasted_iota(jnp.int32, (m, chans), 0) % cols
    windows = [padded[:, a : a + rows].reshape(m, chans) for a in range(3)]
    total = None
    for b in (1, 0, 2):
        part = dot32(windows[0], w_ref[b])
        part = part + dot32(windows[1], w_ref[3 + b])
        part = part + dot32(windows[2], w_ref[6 + b])
        if b == 0:
            part = jnp.where(col == 0, 0.0, pltpu.roll(part, 1, 0))
        elif b == 2:
            part = jnp.where(col == cols - 1, 0.0, pltpu.roll(part, m - 1, 0))
        total = part if total is None else total + part
    return (total / (1.0 + jnp.exp(-total))).astype(bf16)


def fill(padded, video_ref, top_ref, bottom_ref, rows):
    padded[:, 1 : rows + 1] = video_ref[...]
    padded[:, 0] = top_ref[...]
    padded[:, rows + 1] = bottom_ref[...]


def hidden_kernel(video_ref, top_ref, bottom_ref, w_ref, out_ref, padded):
    frames, rows, cols, chans = video_ref.shape
    fill(padded, video_ref, top_ref, bottom_ref, rows)
    out_ref[...] = conv_hidden(padded, w_ref, frames, rows, cols, chans).reshape(out_ref.shape)


def conv_kernel(back_ref, video_ref, top_ref, bottom_ref, earlier_ref, w_ref, wt_ref,
                out_ref, last_ref, padded, hist, stage, acc):
    frames, rows, cols, chans = video_ref.shape
    cells = rows * cols
    fill(padded, video_ref, top_ref, bottom_ref, rows)
    hist[0:2] = earlier_ref[...]
    hist[2:] = conv_hidden(padded, w_ref, frames, rows, cols, chans).reshape(frames, cells, chans)
    for f in range(frames):
        stage[0, f] = hist[back_ref[0, f]]
        stage[1, f] = hist[back_ref[1, f]]
    m = frames * cells
    total = dot32(hist[2:].reshape(m, chans), wt_ref[0])
    total = total + dot32(stage[0].reshape(m, chans), wt_ref[1])
    total = total + dot32(stage[1].reshape(m, chans), wt_ref[2])
    total = total + video_ref[...].reshape(m, chans).astype(f32)
    slots = chans // 128
    for s in range(slots):
        acc[s] = total[:, s * 128 : (s + 1) * 128]
    for f in range(frames):
        for s in range(slots):
            for w in range(0, cols, 2):
                pair = [acc[s, pl.ds(f * cells + w + d, rows, stride=cols), :] for d in range(2)]
                out_ref[f, w * rows : (w + 2) * rows, s * 128 : (s + 1) * 128] = (
                    jnp.concatenate(pair, axis=0).astype(bf16)
                )
    last_ref[...] = hist[frames:]


def spatial_kernel(x_ref, w_ref, out_ref, q_s, k_s, v_s):
    pieces, cells, chans = x_ref.shape
    tm_count = out_ref.shape[0]
    length = pieces * cells
    values = x_ref[...].reshape(length, chans).astype(f32)
    per_group = chans // GROUPS
    sums = jnp.sum(values, axis=0, keepdims=True)
    squares = jnp.sum(values * values, axis=0, keepdims=True)
    both = jnp.concatenate([sums, squares, jnp.zeros((6, chans), f32)], axis=0)
    same = (
        lax.broadcasted_iota(jnp.int32, (chans, chans), 0) // per_group
        == lax.broadcasted_iota(jnp.int32, (chans, chans), 1) // per_group
    ).astype(f32)
    grouped = jnp.dot(both, same, precision=lax.Precision.HIGHEST, preferred_element_type=f32)
    average = grouped[0:1] / (length * per_group)
    spread = grouped[1:2] / (length * per_group) - average * average
    normed = ((values - average) * lax.rsqrt(spread + epsilon)).astype(bf16)
    q_s[...] = dot32(normed, w_ref[0]).astype(bf16)
    k_s[...] = dot32(normed, w_ref[1]).astype(bf16)
    v_s[...] = dot32(normed, w_ref[2]).astype(bf16)
    for r in range(pieces):
        q = q_s[r * cells : (r + 1) * cells]
        logits = lax.dot_general(q, k_s[...], (((1,), (1,)), ((), ())), preferred_element_type=f32)
        logits = logits * chans ** (-0.5)
        raised = jnp.exp(logits - jnp.max(logits, axis=-1, keepdims=True))
        probs = (raised * (1.0 / jnp.sum(raised, axis=-1, keepdims=True))).astype(bf16)
        mix = dot32(probs, v_s[...]).astype(bf16)
        out = (x_ref[r].astype(f32) + dot32(mix, w_ref[3])).astype(bf16)
        out_ref[:, r] = out.reshape(tm_count, cells // tm_count, chans)


def time_kernel(*refs):
    *x_refs, idc_ref, idr_ref, w_ref, out_ref, scr, x_s, q_s, k_s, v_s, m_s = refs
    chunks = len(x_refs)
    frames, ys, chans = out_ref.shape
    slots = chans // 128
    tm_count, pieces = x_refs[0].shape[:2]
    per = frames // tm_count
    for k, x_ref in enumerate(x_refs):
        value = x_ref[...].reshape(tm_count, pieces * ys, chans).astype(f32)
        for t in range(tm_count):
            base = (t * per + k * pieces) * ys
            for s in range(slots):
                scr[s, base : base + pieces * ys] = value[t, :, s * 128 : (s + 1) * 128]
    for y in range(ys):
        x_s[y * frames : (y + 1) * frames] = jnp.concatenate(
            [scr[s, pl.ds(y, frames, stride=ys), :] for s in range(slots)], axis=1
        )
    values = x_s[...]
    average = jnp.mean(values, axis=-1, keepdims=True)
    centered = values - average
    spread = jnp.mean(centered * centered, axis=-1, keepdims=True)
    normed = (centered * lax.rsqrt(spread + epsilon)).astype(bf16)
    q_s[...] = dot32(normed, w_ref[0]).astype(bf16)
    k_s[...] = dot32(normed, w_ref[1]).astype(bf16)
    v_s[...] = dot32(normed, w_ref[2]).astype(bf16)
    g = lax.broadcasted_iota(jnp.int32, (frames, frames), 1)
    f = lax.broadcasted_iota(jnp.int32, (frames, frames), 0)
    allowed = (g <= f) & (idc_ref[...] == idr_ref[...])
    for y in range(ys):
        rows = slice(y * frames, (y + 1) * frames)
        logits = lax.dot_general(
            q_s[rows], k_s[rows], (((1,), (1,)), ((), ())), preferred_element_type=f32
        )
        logits = jnp.where(allowed, logits * chans ** (-0.5), masked_score)
        raised = jnp.exp(logits - jnp.max(logits, axis=-1, keepdims=True))
        probs = (raised * (1.0 / jnp.sum(raised, axis=-1, keepdims=True))).astype(bf16)
        m_s[rows] = dot32(probs, v_s[rows]).astype(bf16)
    out = x_s[...] + dot32(m_s[...], w_ref[3])
    for y in range(ys):
        for s in range(slots):
            scr[s, pl.ds(y, frames, stride=ys), :] = out[
                y * frames : (y + 1) * frames, s * 128 : (s + 1) * 128
            ]
    for s in range(slots):
        out_ref[:, :, s * 128 : (s + 1) * 128] = (
            scr[s].reshape(frames, ys, 128).astype(bf16)
        )


def params():
    return pltpu.CompilerParams(vmem_limit_bytes=VMEM_LIMIT)


def cost(flops, bytes_accessed):
    return pl.CostEstimate(flops=flops, bytes_accessed=bytes_accessed, transcendentals=0)


def block(shape, index):
    return pl.BlockSpec(shape, lambda i: index)


def shards(video, video_ids, w_space, w_time, spatial_attn, time_attn):
    frame_count, rows, cols, chans = video.shape
    tm_count, rows_count = lax.axis_size("tm"), lax.axis_size("rows")
    cells = rows * cols
    per = rows_count
    chunks = frame_count // per
    up = [(i, i + 1) for i in range(rows_count - 1)]
    down = [(j, i) for i, j in up]
    top = lax.ppermute(video[:, rows - 1], "rows", up)
    bottom = lax.ppermute(video[:, 0], "rows", down)

    span = lax.axis_index("tm")
    ids_padded = jnp.concatenate([jnp.full((2,), -1, jnp.int32), video_ids])
    local = lax.dynamic_slice_in_dim(ids_padded, span * frame_count, frame_count + 2)
    slot = jnp.arange(frame_count, dtype=jnp.int32) % per + 2
    one = jnp.where(local[1 : frame_count + 1] == local[2:], slot - 1, slot)
    two = jnp.where(local[:frame_count] == local[2:], slot - 2, one)
    back = jnp.stack([one, two]).reshape(2, chunks, per).transpose(1, 0, 2)

    def hidden_of(index):
        return pl.pallas_call(
            hidden_kernel,
            out_shape=jax.ShapeDtypeStruct((2, cells, chans), bf16),
            grid=(1,),
            in_specs=[
                block((2, rows, cols, chans), (index, 0, 0, 0)),
                block((2, cols, chans), (index, 0, 0)),
                block((2, cols, chans), (index, 0, 0)),
                block((9, chans, chans), (0, 0, 0)),
            ],
            scratch_shapes=[pltpu.VMEM((2, rows + 2, cols, chans), bf16)],
            compiler_params=params(),
            cost_estimate=cost(2 * 2 * 9 * cells * chans * chans, 18 * chans * chans),
            name="hidden_two",
        )(video, top, bottom, w_space)

    def conv_of(k, earlier):
        m = per * cells
        return pl.pallas_call(
            conv_kernel,
            out_shape=(
                jax.ShapeDtypeStruct((per, cells, chans), bf16),
                jax.ShapeDtypeStruct((2, cells, chans), bf16),
            ),
            grid=(1,),
            in_specs=[
                pl.BlockSpec(memory_space=pltpu.SMEM),
                block((per, rows, cols, chans), (k, 0, 0, 0)),
                block((per, cols, chans), (k, 0, 0)),
                block((per, cols, chans), (k, 0, 0)),
                block((2, cells, chans), (0, 0, 0)),
                block((9, chans, chans), (0, 0, 0)),
                block((3, chans, chans), (0, 0, 0)),
            ],
            scratch_shapes=[
                pltpu.VMEM((per, rows + 2, cols, chans), bf16),
                pltpu.VMEM((per + 2, cells, chans), bf16),
                pltpu.VMEM((2, per, cells, chans), bf16),
                pltpu.VMEM((chans // 128, m, 128), f32),
            ],
            compiler_params=params(),
            cost_estimate=cost(2 * 12 * m * chans * chans, 24 * chans * chans + 6 * m * chans),
            name="conv_chunk",
        )(back[k], video, top, bottom, earlier, w_space, w_time)

    def exchange(piece):
        return lax.all_to_all(piece, "rows", split_axis=0, concat_axis=0, tiled=True)

    def spatial_of(x):
        length = rows_count * cells
        return pl.pallas_call(
            spatial_kernel,
            out_shape=jax.ShapeDtypeStruct(
                (tm_count, rows_count, cells // tm_count, chans), bf16
            ),
            scratch_shapes=[pltpu.VMEM((length, chans), bf16)] * 3,
            compiler_params=params(),
            cost_estimate=cost(
                2 * 4 * length * chans * chans + 4 * length * length * chans,
                8 * chans * chans + 4 * length * chans,
            ),
            name="spatial_frame",
        )(x, spatial_attn)

    carry = hidden_of(per // 2 - 1)
    conv = [None] * chunks
    for k in range(1, chunks):
        conv[k], carry = conv_of(k, carry)
    forward = [(i, i + 1) for i in range(tm_count - 1)]
    conv[0], _ = conv_of(0, lax.ppermute(carry, "tm", forward))
    arrived = [None] * chunks
    for k in [*range(1, chunks), 0]:
        frame = spatial_of(exchange(conv[k]))
        outgoing = frame.reshape(tm_count * rows_count, cells // tm_count, chans)
        arrived[k] = lax.all_to_all(
            outgoing, ("tm", "rows"), split_axis=0, concat_axis=0, tiled=True
        )
    slab = cols // tm_count
    frame_total = tm_count * frame_count
    inputs = [x.reshape(tm_count, rows_count, slab, rows, chans) for x in arrived]
    m = frame_total * rows
    out = pl.pallas_call(
        time_kernel,
        out_shape=jax.ShapeDtypeStruct((frame_total, rows, slab * chans), bf16),
        grid=(slab,),
        in_specs=[
            pl.BlockSpec((tm_count, rows_count, None, rows, chans), lambda c: (0, 0, c, 0, 0))
            for _ in inputs
        ]
        + [
            pl.BlockSpec((frame_total, 1), lambda c: (0, 0)),
            pl.BlockSpec((1, frame_total), lambda c: (0, 0)),
            pl.BlockSpec((4, chans, chans), lambda c: (0, 0, 0)),
        ],
        out_specs=pl.BlockSpec((frame_total, rows, chans), lambda c: (0, 0, c)),
        scratch_shapes=[
            pltpu.VMEM((chans // 128, m, 128), f32),
            pltpu.VMEM((m, chans), f32),
        ]
        + [pltpu.VMEM((m, chans), bf16)] * 4,
        compiler_params=params(),
        name="time_cells",
    )(*inputs, video_ids.reshape(-1, 1), video_ids.reshape(1, -1), time_attn)
    return out.reshape(frame_total, rows, slab, chans)


def solution(mesh):
    in_specs = (P("tm", "rows", None, None), P(), P(), P(), P(), P())
    out_specs = P(None, "rows", "tm", None)
    return jax.shard_map(shards, mesh=mesh, in_specs=in_specs, out_specs=out_specs, check_vma=False)
```

```python
import jax
import jax.numpy as jnp
from jax import lax
from jax.experimental import pallas as pl
from jax.experimental.pallas import tpu as pltpu
from jax.sharding import PartitionSpec as P

GROUPS = 32
epsilon = 1e-06
masked_score = -1e30
f32, bf16 = jnp.float32, jnp.bfloat16
VMEM_LIMIT = 60 * 1024 * 1024


def dot32(a, b):
    return jnp.dot(a, b, preferred_element_type=f32)


def conv_hidden(padded, w_ref, frames, rows, cols, chans):
    m = frames * rows * cols
    col = lax.broadcasted_iota(jnp.int32, (m, chans), 0) % cols
    windows = [padded[:, a : a + rows].reshape(m, chans) for a in range(3)]
    total = None
    for b in (1, 0, 2):
        part = dot32(windows[0], w_ref[b])
        part = part + dot32(windows[1], w_ref[3 + b])
        part = part + dot32(windows[2], w_ref[6 + b])
        if b == 0:
            part = jnp.where(col == 0, 0.0, pltpu.roll(part, 1, 0))
        elif b == 2:
            part = jnp.where(col == cols - 1, 0.0, pltpu.roll(part, m - 1, 0))
        total = part if total is None else total + part
    return (total / (1.0 + jnp.exp(-total))).astype(bf16)


def fill(padded, video_ref, top_ref, bottom_ref, rows):
    padded[:, 1 : rows + 1] = video_ref[...]
    padded[:, 0] = top_ref[...]
    padded[:, rows + 1] = bottom_ref[...]


def hidden_kernel(video_ref, top_ref, bottom_ref, w_ref, out_ref, padded):
    frames, rows, cols, chans = video_ref.shape
    fill(padded, video_ref, top_ref, bottom_ref, rows)
    out_ref[...] = conv_hidden(padded, w_ref, frames, rows, cols, chans).reshape(out_ref.shape)


def conv_kernel(back_ref, video_ref, top_ref, bottom_ref, earlier_ref, w_ref, wt_ref, after_ref,
                out_ref, last_ref, padded, hist, stage, acc):
    frames, rows, cols, chans = video_ref.shape
    cells = rows * cols
    fill(padded, video_ref, top_ref, bottom_ref, rows)
    hist[0:2] = earlier_ref[...]
    hist[2:] = conv_hidden(padded, w_ref, frames, rows, cols, chans).reshape(frames, cells, chans)
    for f in range(frames):
        stage[0, f] = hist[back_ref[0, f]]
        stage[1, f] = hist[back_ref[1, f]]
    m = frames * cells
    total = dot32(hist[2:].reshape(m, chans), wt_ref[0])
    total = total + dot32(stage[0].reshape(m, chans), wt_ref[1])
    total = total + dot32(stage[1].reshape(m, chans), wt_ref[2])
    total = total + video_ref[...].reshape(m, chans).astype(f32)
    slots = chans // 128
    for s in range(slots):
        acc[s] = total[:, s * 128 : (s + 1) * 128]
    for f in range(frames):
        place = back_ref[2, f]
        for s in range(slots):
            for w in range(0, cols, 2):
                pair = [acc[s, pl.ds(f * cells + w + d, rows, stride=cols), :] for d in range(2)]
                out_ref[place, w * rows : (w + 2) * rows, s * 128 : (s + 1) * 128] = (
                    jnp.concatenate(pair, axis=0).astype(bf16)
                )
    last_ref[...] = hist[frames:]


def spatial_kernel(source_ref, *refs):
    *parts, w_ref, after_ref, out_ref, x_ref, q_s, k_s, v_s = refs
    pieces, cells, chans = x_ref.shape
    for j, part in enumerate(parts):
        x_ref[j] = part[0]
    tm_count = out_ref.shape[0]
    length = pieces * cells
    values = x_ref[...].reshape(length, chans).astype(f32)
    per_group = chans // GROUPS
    sums = jnp.sum(values, axis=0, keepdims=True)
    squares = jnp.sum(values * values, axis=0, keepdims=True)
    both = jnp.concatenate([sums, squares, jnp.zeros((6, chans), f32)], axis=0)
    same = (
        lax.broadcasted_iota(jnp.int32, (chans, chans), 0) // per_group
        == lax.broadcasted_iota(jnp.int32, (chans, chans), 1) // per_group
    ).astype(f32)
    grouped = jnp.dot(both, same, precision=lax.Precision.HIGHEST, preferred_element_type=f32)
    average = grouped[0:1] / (length * per_group)
    spread = grouped[1:2] / (length * per_group) - average * average
    normed = ((values - average) * lax.rsqrt(spread + epsilon)).astype(bf16)
    q_s[...] = dot32(normed, w_ref[0]).astype(bf16)
    k_s[...] = dot32(normed, w_ref[1]).astype(bf16)
    v_s[...] = dot32(normed, w_ref[2]).astype(bf16)
    for r in range(pieces):
        q = q_s[r * cells : (r + 1) * cells]
        logits = lax.dot_general(q, k_s[...], (((1,), (1,)), ((), ())), preferred_element_type=f32)
        logits = logits * chans ** (-0.5)
        raised = jnp.exp(logits - jnp.max(logits, axis=-1, keepdims=True))
        probs = (raised * (1.0 / jnp.sum(raised, axis=-1, keepdims=True))).astype(bf16)
        mix = dot32(probs, v_s[...]).astype(bf16)
        out = (x_ref[r].astype(f32) + dot32(mix, w_ref[3])).astype(bf16)
        out_ref[:, source_ref[r]] = out.reshape(tm_count, cells // tm_count, chans)


def time_kernel(*refs):
    *x_refs, idc_ref, idr_ref, w_ref, out_ref, scr, x_s, q_s, k_s, v_s, m_s = refs
    chunks = len(x_refs)
    frames, ys, chans = out_ref.shape
    slots = chans // 128
    tm_count, pieces = x_refs[0].shape[:2]
    per = frames // tm_count
    for k, x_ref in enumerate(x_refs):
        value = x_ref[...].reshape(tm_count, pieces * ys, chans).astype(f32)
        for t in range(tm_count):
            base = (t * per + k * pieces) * ys
            for s in range(slots):
                scr[s, base : base + pieces * ys] = value[t, :, s * 128 : (s + 1) * 128]
    for y in range(ys):
        x_s[y * frames : (y + 1) * frames] = jnp.concatenate(
            [scr[s, pl.ds(y, frames, stride=ys), :] for s in range(slots)], axis=1
        )
    values = x_s[...]
    average = jnp.mean(values, axis=-1, keepdims=True)
    centered = values - average
    spread = jnp.mean(centered * centered, axis=-1, keepdims=True)
    normed = (centered * lax.rsqrt(spread + epsilon)).astype(bf16)
    q_s[...] = dot32(normed, w_ref[0]).astype(bf16)
    k_s[...] = dot32(normed, w_ref[1]).astype(bf16)
    v_s[...] = dot32(normed, w_ref[2]).astype(bf16)
    g = lax.broadcasted_iota(jnp.int32, (frames, frames), 1)
    f = lax.broadcasted_iota(jnp.int32, (frames, frames), 0)
    allowed = (g <= f) & (idc_ref[...] == idr_ref[...])
    for y in range(ys):
        rows = slice(y * frames, (y + 1) * frames)
        logits = lax.dot_general(
            q_s[rows], k_s[rows], (((1,), (1,)), ((), ())), preferred_element_type=f32
        )
        logits = jnp.where(allowed, logits * chans ** (-0.5), masked_score)
        raised = jnp.exp(logits - jnp.max(logits, axis=-1, keepdims=True))
        probs = (raised * (1.0 / jnp.sum(raised, axis=-1, keepdims=True))).astype(bf16)
        m_s[rows] = dot32(probs, v_s[rows]).astype(bf16)
    out = x_s[...] + dot32(m_s[...], w_ref[3])
    for y in range(ys):
        for s in range(slots):
            scr[s, pl.ds(y, frames, stride=ys), :] = out[
                y * frames : (y + 1) * frames, s * 128 : (s + 1) * 128
            ]
    for s in range(slots):
        out_ref[:, :, s * 128 : (s + 1) * 128] = (
            scr[s].reshape(frames, ys, 128).astype(bf16)
        )


def params():
    return pltpu.CompilerParams(vmem_limit_bytes=VMEM_LIMIT)


def cost(flops, bytes_accessed):
    return pl.CostEstimate(flops=flops, bytes_accessed=bytes_accessed, transcendentals=0)


def block(shape, index):
    return pl.BlockSpec(shape, lambda i: index)


def shards(video, video_ids, w_space, w_time, spatial_attn, time_attn):
    frame_count, rows, cols, chans = video.shape
    tm_count, rows_count = lax.axis_size("tm"), lax.axis_size("rows")
    cells = rows * cols
    per = rows_count
    chunks = frame_count // per
    up = [(i, i + 1) for i in range(rows_count - 1)]
    down = [(j, i) for i, j in up]
    top = lax.ppermute(video[:, rows - 1], "rows", up)
    bottom = lax.ppermute(video[:, 0], "rows", down)

    span = lax.axis_index("tm")
    ids_padded = jnp.concatenate([jnp.full((2,), -1, jnp.int32), video_ids])
    local = lax.dynamic_slice_in_dim(ids_padded, span * frame_count, frame_count + 2)
    slot = jnp.arange(frame_count, dtype=jnp.int32) % per + 2
    one = jnp.where(local[1 : frame_count + 1] == local[2:], slot - 1, slot)
    two = jnp.where(local[:frame_count] == local[2:], slot - 2, one)
    me = lax.axis_index("rows")
    place = (jnp.arange(frame_count, dtype=jnp.int32) - me) % per
    back = jnp.stack([one, two, place]).reshape(3, chunks, per).transpose(1, 0, 2)
    source = (me - jnp.arange(rows_count, dtype=jnp.int32)) % rows_count

    def hidden_of(index):
        return pl.pallas_call(
            hidden_kernel,
            out_shape=jax.ShapeDtypeStruct((2, cells, chans), bf16),
            grid=(1,),
            in_specs=[
                block((2, rows, cols, chans), (index, 0, 0, 0)),
                block((2, cols, chans), (index, 0, 0)),
                block((2, cols, chans), (index, 0, 0)),
                block((9, chans, chans), (0, 0, 0)),
            ],
            scratch_shapes=[pltpu.VMEM((2, rows + 2, cols, chans), bf16)],
            compiler_params=params(),
            cost_estimate=cost(2 * 2 * 9 * cells * chans * chans, 18 * chans * chans),
            name="hidden_two",
        )(video, top, bottom, w_space)

    def conv_of(k, earlier, after):
        m = per * cells
        return pl.pallas_call(
            conv_kernel,
            out_shape=(
                jax.ShapeDtypeStruct((per, cells, chans), bf16),
                jax.ShapeDtypeStruct((2, cells, chans), bf16),
            ),
            grid=(1,),
            in_specs=[
                pl.BlockSpec(memory_space=pltpu.SMEM),
                block((per, rows, cols, chans), (k, 0, 0, 0)),
                block((per, cols, chans), (k, 0, 0)),
                block((per, cols, chans), (k, 0, 0)),
                block((2, cells, chans), (0, 0, 0)),
                block((9, chans, chans), (0, 0, 0)),
                block((3, chans, chans), (0, 0, 0)),
                pl.BlockSpec(memory_space=pl.ANY),
            ],
            scratch_shapes=[
                pltpu.VMEM((per, rows + 2, cols, chans), bf16),
                pltpu.VMEM((per + 2, cells, chans), bf16),
                pltpu.VMEM((2, per, cells, chans), bf16),
                pltpu.VMEM((chans // 128, m, 128), f32),
            ],
            compiler_params=params(),
            cost_estimate=cost(2 * 12 * m * chans * chans, 24 * chans * chans + 6 * m * chans),
            name="conv_chunk",
        )(back[k], video, top, bottom, earlier, w_space, w_time, after)

    def exchange(piece):
        parts = [piece]
        for shift in range(1, rows_count):
            route = [(i, (i + shift) % rows_count) for i in range(rows_count)]
            parts.append(lax.ppermute(piece[shift : shift + 1], "rows", route))
        return parts

    def spatial_of(parts, after):
        length = rows_count * cells
        return pl.pallas_call(
            spatial_kernel,
            out_shape=jax.ShapeDtypeStruct(
                (tm_count, rows_count, cells // tm_count, chans), bf16
            ),
            grid=(1,),
            in_specs=[pl.BlockSpec(memory_space=pltpu.SMEM)]
            + [block((1, cells, chans), (0, 0, 0)) for _ in parts]
            + [block((4, chans, chans), (0, 0, 0)), pl.BlockSpec(memory_space=pl.ANY)],
            scratch_shapes=[pltpu.VMEM((rows_count, cells, chans), bf16)]
            + [pltpu.VMEM((length, chans), bf16)] * 3,
            compiler_params=params(),
            cost_estimate=cost(
                2 * 4 * length * chans * chans + 4 * length * length * chans,
                8 * chans * chans + 4 * length * chans,
            ),
            name="spatial_frame",
        )(source, *parts, spatial_attn, after)

    carry = hidden_of(per // 2 - 1)
    forward = [(i, i + 1) for i in range(tm_count - 1)]
    order = [*range(1, chunks), 0]
    arrived = [None] * chunks

    def conv_step(k, carry, after):
        if k == 0:
            carry = lax.ppermute(carry, "tm", forward)
        out, carry = conv_of(k, carry, after)
        return exchange(out), carry

    parts = [None] * chunks
    parts[order[0]], carry = conv_step(order[0], carry, carry)
    parts[order[1]], carry = conv_step(order[1], carry, carry)
    after = carry
    for step, k in enumerate(order):
        frame = spatial_of(parts[k], after)
        outgoing = frame.reshape(tm_count * rows_count, cells // tm_count, chans)
        arrived[k] = lax.all_to_all(
            outgoing, ("tm", "rows"), split_axis=0, concat_axis=0, tiled=True
        )
        after = frame
        if step + 2 < chunks:
            later = order[step + 2]
            parts[later], carry = conv_step(later, carry, frame)
            after = carry
    slab = cols // tm_count
    frame_total = tm_count * frame_count
    inputs = [x.reshape(tm_count, rows_count, slab, rows, chans) for x in arrived]
    m = frame_total * rows
    out = pl.pallas_call(
        time_kernel,
        out_shape=jax.ShapeDtypeStruct((frame_total, rows, slab * chans), bf16),
        grid=(slab,),
        in_specs=[
            pl.BlockSpec((tm_count, rows_count, None, rows, chans), lambda c: (0, 0, c, 0, 0))
            for _ in inputs
        ]
        + [
            pl.BlockSpec((frame_total, 1), lambda c: (0, 0)),
            pl.BlockSpec((1, frame_total), lambda c: (0, 0)),
            pl.BlockSpec((4, chans, chans), lambda c: (0, 0, 0)),
        ],
        out_specs=pl.BlockSpec((frame_total, rows, chans), lambda c: (0, 0, c)),
        scratch_shapes=[
            pltpu.VMEM((chans // 128, m, 128), f32),
            pltpu.VMEM((m, chans), f32),
        ]
        + [pltpu.VMEM((m, chans), bf16)] * 4,
        compiler_params=params(),
        name="time_cells",
    )(*inputs, video_ids.reshape(-1, 1), video_ids.reshape(1, -1), time_attn)
    return out.reshape(frame_total, rows, slab, chans)


def solution(mesh):
    in_specs = (P("tm", "rows", None, None), P(), P(), P(), P(), P())
    out_specs = P(None, "rows", "tm", None)
    return jax.shard_map(shards, mesh=mesh, in_specs=in_specs, out_specs=out_specs, check_vma=False)
```

```python
import functools

import jax
import jax.numpy as jnp
from jax import lax
from jax.experimental import pallas as pl
from jax.experimental.pallas import tpu as pltpu
from jax.sharding import PartitionSpec as P

GROUPS = 32
epsilon = 1e-06
masked_score = -1e30
f32, bf16 = jnp.float32, jnp.bfloat16


def dot32(a, b):
    return jnp.dot(a, b, preferred_element_type=f32)


def conv_hidden(padded, w_ref, frames, rows, cols, chans):
    m = frames * rows * cols
    col = lax.broadcasted_iota(jnp.int32, (m, chans), 0) % cols
    windows = [padded[:, a : a + rows].reshape(m, chans) for a in range(3)]
    total = None
    for b in (1, 0, 2):
        part = dot32(windows[0], w_ref[b])
        part = part + dot32(windows[1], w_ref[3 + b])
        part = part + dot32(windows[2], w_ref[6 + b])
        if b == 0:
            part = jnp.where(col == 0, 0.0, pltpu.roll(part, 1, 0))
        elif b == 2:
            part = jnp.where(col == cols - 1, 0.0, pltpu.roll(part, m - 1, 0))
        total = part if total is None else total + part
    return (total / (1.0 + jnp.exp(-total))).astype(bf16)


def fill(padded, video_ref, top_ref, bottom_ref, rows):
    padded[:, 1 : rows + 1] = video_ref[...]
    padded[:, 0] = top_ref[...]
    padded[:, rows + 1] = bottom_ref[...]


def hidden_kernel(video_ref, top_ref, bottom_ref, w_ref, out_ref, padded):
    frames, rows, cols, chans = video_ref.shape
    fill(padded, video_ref, top_ref, bottom_ref, rows)
    out_ref[...] = conv_hidden(padded, w_ref, frames, rows, cols, chans).reshape(out_ref.shape)


def conv_kernel(back_ref, video_ref, top_ref, bottom_ref, earlier_ref, w_ref, wt_ref, after_ref,
                out_ref, last_ref, padded, hist, stage, acc):
    frames, rows, cols, chans = video_ref.shape
    cells = rows * cols
    fill(padded, video_ref, top_ref, bottom_ref, rows)
    hist[0:2] = earlier_ref[...]
    hist[2:] = conv_hidden(padded, w_ref, frames, rows, cols, chans).reshape(frames, cells, chans)
    for f in range(frames):
        stage[0, f] = hist[back_ref[0, f]]
        stage[1, f] = hist[back_ref[1, f]]
    m = frames * cells
    total = dot32(hist[2:].reshape(m, chans), wt_ref[0])
    total = total + dot32(stage[0].reshape(m, chans), wt_ref[1])
    total = total + dot32(stage[1].reshape(m, chans), wt_ref[2])
    total = total + video_ref[...].reshape(m, chans).astype(f32)
    slots = chans // 128
    for s in range(slots):
        acc[s] = total[:, s * 128 : (s + 1) * 128]
    for f in range(frames):
        place = back_ref[2, f]
        for s in range(slots):
            for w in range(0, cols, 2):
                pair = [acc[s, pl.ds(f * cells + w + d, rows, stride=cols), :] for d in range(2)]
                out_ref[place, w * rows : (w + 2) * rows, s * 128 : (s + 1) * 128] = (
                    jnp.concatenate(pair, axis=0).astype(bf16)
                )
    last_ref[...] = hist[frames:]


def spatial_kernel(source_ref, *refs):
    out_ref, x_ref, q_s, k_s, v_s = refs[-5:]
    pieces, cells, chans = x_ref.shape
    parts, w_ref = refs[:pieces], refs[pieces]
    for j, part in enumerate(parts):
        x_ref[j] = part[0]
    tm_count = out_ref.shape[0]
    length = pieces * cells
    values = x_ref[...].reshape(length, chans).astype(f32)
    per_group = chans // GROUPS
    sums = jnp.sum(values, axis=0, keepdims=True)
    squares = jnp.sum(values * values, axis=0, keepdims=True)
    both = jnp.concatenate([sums, squares, jnp.zeros((6, chans), f32)], axis=0)
    same = (
        lax.broadcasted_iota(jnp.int32, (chans, chans), 0) // per_group
        == lax.broadcasted_iota(jnp.int32, (chans, chans), 1) // per_group
    ).astype(f32)
    grouped = jnp.dot(both, same, precision=lax.Precision.HIGHEST, preferred_element_type=f32)
    average = grouped[0:1] / (length * per_group)
    spread = grouped[1:2] / (length * per_group) - average * average
    normed = ((values - average) * lax.rsqrt(spread + epsilon)).astype(bf16)
    q_s[...] = dot32(normed, w_ref[0]).astype(bf16)
    k_s[...] = dot32(normed, w_ref[1]).astype(bf16)
    v_s[...] = dot32(normed, w_ref[2]).astype(bf16)
    for r in range(pieces):
        q = q_s[r * cells : (r + 1) * cells]
        logits = lax.dot_general(q, k_s[...], (((1,), (1,)), ((), ())), preferred_element_type=f32)
        logits = logits * chans ** (-0.5)
        raised = jnp.exp(logits - jnp.max(logits, axis=-1, keepdims=True))
        probs = (raised * (1.0 / jnp.sum(raised, axis=-1, keepdims=True))).astype(bf16)
        mix = dot32(probs, v_s[...]).astype(bf16)
        out = (x_ref[r].astype(f32) + dot32(mix, w_ref[3])).astype(bf16)
        out_ref[:, source_ref[r]] = out.reshape(tm_count, cells // tm_count, chans)


def time_kernel(places, *refs):
    *x_refs, idc_ref, idr_ref, w_ref, out_ref, scr, x_s, q_s, k_s, v_s, m_s = refs
    frames, ys, chans = out_ref.shape
    slots = chans // 128
    tm_count, pieces = x_refs[0].shape[:2]
    per = frames // tm_count
    arrived = [(k, x_ref, i) for x_ref, ks in zip(x_refs, places) for i, k in enumerate(ks)]
    for k, x_ref, i in arrived:
        value = x_ref[:, :, i].reshape(tm_count, pieces * ys, chans).astype(f32)
        for t in range(tm_count):
            base = (t * per + k * pieces) * ys
            for s in range(slots):
                scr[s, base : base + pieces * ys] = value[t, :, s * 128 : (s + 1) * 128]
    for y in range(ys):
        x_s[y * frames : (y + 1) * frames] = jnp.concatenate(
            [scr[s, pl.ds(y, frames, stride=ys), :] for s in range(slots)], axis=1
        )
    values = x_s[...]
    average = jnp.mean(values, axis=-1, keepdims=True)
    centered = values - average
    spread = jnp.mean(centered * centered, axis=-1, keepdims=True)
    normed = (centered * lax.rsqrt(spread + epsilon)).astype(bf16)
    q_s[...] = dot32(normed, w_ref[0]).astype(bf16)
    k_s[...] = dot32(normed, w_ref[1]).astype(bf16)
    v_s[...] = dot32(normed, w_ref[2]).astype(bf16)
    g = lax.broadcasted_iota(jnp.int32, (frames, frames), 1)
    f = lax.broadcasted_iota(jnp.int32, (frames, frames), 0)
    allowed = (g <= f) & (idc_ref[...] == idr_ref[...])
    for y in range(ys):
        rows = slice(y * frames, (y + 1) * frames)
        logits = lax.dot_general(
            q_s[rows], k_s[rows], (((1,), (1,)), ((), ())), preferred_element_type=f32
        )
        logits = jnp.where(allowed, logits * chans ** (-0.5), masked_score)
        raised = jnp.exp(logits - jnp.max(logits, axis=-1, keepdims=True))
        probs = (raised * (1.0 / jnp.sum(raised, axis=-1, keepdims=True))).astype(bf16)
        m_s[rows] = dot32(probs, v_s[rows]).astype(bf16)
    out = x_s[...] + dot32(m_s[...], w_ref[3])
    for y in range(ys):
        for s in range(slots):
            scr[s, pl.ds(y, frames, stride=ys), :] = out[
                y * frames : (y + 1) * frames, s * 128 : (s + 1) * 128
            ]
    for s in range(slots):
        out_ref[:, :, s * 128 : (s + 1) * 128] = (
            scr[s].reshape(frames, ys, 128).astype(bf16)
        )


def params(mib):
    return pltpu.CompilerParams(vmem_limit_bytes=mib * 1024 * 1024)


def cost(flops, bytes_accessed):
    return pl.CostEstimate(flops=flops, bytes_accessed=bytes_accessed, transcendentals=0)


def block(shape, index):
    return pl.BlockSpec(shape, lambda i: index)


def behind_kernel(*refs):
    pass


def behind(value, others):
    spec = pl.BlockSpec(memory_space=pl.ANY)
    return pl.pallas_call(
        behind_kernel,
        out_shape=jax.ShapeDtypeStruct(value.shape, value.dtype),
        in_specs=[spec] * (1 + len(others)),
        out_specs=spec,
        input_output_aliases={0: 0},
        name="behind",
    )(value, *others)


def shards(video, video_ids, w_space, w_time, spatial_attn, time_attn):
    frame_count, rows, cols, chans = video.shape
    tm_count, rows_count = lax.axis_size("tm"), lax.axis_size("rows")
    cells = rows * cols
    per = rows_count
    chunks = frame_count // per
    up = [(i, i + 1) for i in range(rows_count - 1)]
    down = [(j, i) for i, j in up]
    top = lax.ppermute(video[:, rows - 1], "rows", up)
    bottom = lax.ppermute(video[:, 0], "rows", down)

    span = lax.axis_index("tm")
    ids_padded = jnp.concatenate([jnp.full((2,), -1, jnp.int32), video_ids])
    local = lax.dynamic_slice_in_dim(ids_padded, span * frame_count, frame_count + 2)
    slot = jnp.arange(frame_count, dtype=jnp.int32) % per + 2
    one = jnp.where(local[1 : frame_count + 1] == local[2:], slot - 1, slot)
    two = jnp.where(local[:frame_count] == local[2:], slot - 2, one)
    me = lax.axis_index("rows")
    place = (jnp.arange(frame_count, dtype=jnp.int32) - me) % per
    back = jnp.stack([one, two, place]).reshape(3, chunks, per).transpose(1, 0, 2)
    source = (me - jnp.arange(rows_count, dtype=jnp.int32)) % rows_count

    def hidden_of(index):
        return pl.pallas_call(
            hidden_kernel,
            out_shape=jax.ShapeDtypeStruct((2, cells, chans), bf16),
            grid=(1,),
            in_specs=[
                block((2, rows, cols, chans), (index, 0, 0, 0)),
                block((2, cols, chans), (index, 0, 0)),
                block((2, cols, chans), (index, 0, 0)),
                block((9, chans, chans), (0, 0, 0)),
            ],
            scratch_shapes=[pltpu.VMEM((2, rows + 2, cols, chans), bf16)],
            compiler_params=params(28),
            cost_estimate=cost(2 * 2 * 9 * cells * chans * chans, 18 * chans * chans),
            name="hidden_two",
        )(video, top, bottom, w_space)

    def conv_of(k, earlier, after):
        m = per * cells
        return pl.pallas_call(
            conv_kernel,
            out_shape=(
                jax.ShapeDtypeStruct((per, cells, chans), bf16),
                jax.ShapeDtypeStruct((2, cells, chans), bf16),
            ),
            grid=(1,),
            in_specs=[
                pl.BlockSpec(memory_space=pltpu.SMEM),
                block((per, rows, cols, chans), (k, 0, 0, 0)),
                block((per, cols, chans), (k, 0, 0)),
                block((per, cols, chans), (k, 0, 0)),
                block((2, cells, chans), (0, 0, 0)),
                block((9, chans, chans), (0, 0, 0)),
                block((3, chans, chans), (0, 0, 0)),
                pl.BlockSpec(memory_space=pl.ANY),
            ],
            scratch_shapes=[
                pltpu.VMEM((per, rows + 2, cols, chans), bf16),
                pltpu.VMEM((per + 2, cells, chans), bf16),
                pltpu.VMEM((2, per, cells, chans), bf16),
                pltpu.VMEM((chans // 128, m, 128), f32),
            ],
            compiler_params=params(40),
            cost_estimate=cost(2 * 12 * m * chans * chans, 24 * chans * chans + 6 * m * chans),
            name="conv_chunk",
        )(back[k], video, top, bottom, earlier, w_space, w_time, after)

    def exchange(piece):
        parts = [piece]
        for shift in range(1, rows_count):
            route = [(i, (i + shift) % rows_count) for i in range(rows_count)]
            parts.append(lax.ppermute(piece[shift : shift + 1], "rows", route))
        return parts

    def spatial_of(parts, after):
        length = rows_count * cells
        return pl.pallas_call(
            spatial_kernel,
            out_shape=jax.ShapeDtypeStruct(
                (tm_count, rows_count, cells // tm_count, chans), bf16
            ),
            grid=(1,),
            in_specs=[pl.BlockSpec(memory_space=pltpu.SMEM)]
            + [block((1, cells, chans), (0, 0, 0)) for _ in parts]
            + [block((4, chans, chans), (0, 0, 0))]
            + [pl.BlockSpec(memory_space=pl.ANY) for _ in after],
            scratch_shapes=[pltpu.VMEM((rows_count, cells, chans), bf16)]
            + [pltpu.VMEM((length, chans), bf16)] * 3,
            compiler_params=params(28),
            cost_estimate=cost(
                2 * 4 * length * chans * chans + 4 * length * length * chans,
                8 * chans * chans + 4 * length * chans,
            ),
            name="spatial_frame",
        )(source, *parts, spatial_attn, *after)

    carry = hidden_of(per // 2 - 1)
    forward = [(i, i + 1) for i in range(tm_count - 1)]
    order = [*range(1, chunks), 0]
    arrived = [None] * chunks

    def conv_step(k, carry, after):
        out, carry = conv_of(k, carry, after)
        return exchange(out), carry

    slab = cols // tm_count
    frame_total = tm_count * frame_count
    m = frame_total * rows

    def spread(frames):
        outgoing = jnp.stack(
            [frame.reshape(tm_count * rows_count, -1, chans) for frame in frames], axis=1
        ).reshape(tm_count * rows_count, -1, chans)
        landed = lax.all_to_all(
            outgoing, ("tm", "rows"), split_axis=0, concat_axis=0, tiled=True
        )
        return landed.reshape(tm_count, rows_count, len(frames), slab, rows, chans)

    parts = [None] * chunks
    for k in order[:-1]:
        parts[k], carry = conv_step(k, carry, carry)
    handed = lax.ppermute(carry, "tm", forward)
    ready = [carry] if chunks < 3 else [carry, *parts[order[-3]][1:]]
    first = spatial_of(parts[order[0]], ready)
    parts[0], carry = conv_step(0, handed, first)
    frames, after = [first], carry
    for k in order[1:]:
        after = spatial_of(parts[k], [after])
        frames.append(after)
    if chunks > 2:
        frames[0] = behind(frames[0], [handed, *parts[order[-2]][1:]])
        frames[1] = behind(frames[1], parts[0][1:])
    groups = [[i] for i in range(chunks - 2)] + [[chunks - 2, chunks - 1]]
    inputs = [spread([frames[i] for i in group]) for group in groups]
    places = [[order[i] for i in group] for group in groups]
    out = pl.pallas_call(
        functools.partial(time_kernel, places),
        out_shape=jax.ShapeDtypeStruct((frame_total, rows, slab * chans), bf16),
        grid=(slab,),
        in_specs=[
            pl.BlockSpec(
                (tm_count, rows_count, x.shape[2], None, rows, chans),
                lambda c: (0, 0, 0, c, 0, 0),
            )
            for x in inputs
        ]
        + [
            pl.BlockSpec((frame_total, 1), lambda c: (0, 0)),
            pl.BlockSpec((1, frame_total), lambda c: (0, 0)),
            pl.BlockSpec((4, chans, chans), lambda c: (0, 0, 0)),
        ],
        out_specs=pl.BlockSpec((frame_total, rows, chans), lambda c: (0, 0, c)),
        scratch_shapes=[
            pltpu.VMEM((chans // 128, m, 128), f32),
            pltpu.VMEM((m, chans), f32),
        ]
        + [pltpu.VMEM((m, chans), bf16)] * 4,
        compiler_params=params(60),
        name="time_cells",
    )(*inputs, video_ids.reshape(-1, 1), video_ids.reshape(1, -1), time_attn)
    return out.reshape(frame_total, rows, slab, chans)


def solution(mesh):
    in_specs = (P("tm", "rows", None, None), P(), P(), P(), P(), P())
    out_specs = P(None, "rows", "tm", None)
    return jax.shard_map(shards, mesh=mesh, in_specs=in_specs, out_specs=out_specs, check_vma=False)
```
